256 devices in a mesh: section: 8 (over z), expert: 32 (over x, y, core).
Axes of the slice: x: 4, y: 4, z: 8, core: 2. Of those that a mesh axis runs over, the one named last changes fastest.
Arguments:
- grad_out: bfloat16 [4096, 4096], P('expert', 'section'), may hold values from -6 to 6
- probs: float32 [4096, 8], P('expert'), may hold values from 0.05 to 0.4
- expert_ids: int32 [4096, 8], P('expert'), may hold values from 0 to 63, all different within a row; in each aligned block of 128 rows (0 to 127, 128 to 255, ...) at most 24 rows name the same one
- w_gate: bfloat16 [64, 1536, 4096], P('expert', 'section'), may hold values from -0.09375 to 0.09375
- w_up: bfloat16 [64, 1536, 4096], P('expert', 'section'), may hold values from -0.09375 to 0.09375
- w_down: bfloat16 [64, 1536, 4096], P('expert', 'section'), may hold values from -0.15625 to 0.15625
- saved_gate: bfloat16 [64, 1536, 768], P('expert', 'section'), may hold values from -3 to 3
- saved_up: bfloat16 [64, 1536, 768], P('expert', 'section'), may hold values from -3 to 3
Outputs:
- grad_in: bfloat16 [4096, 4096], P('expert', 'section')
- grad_probs: bfloat16 [4096, 8], P('expert')
The draws below stay inside these ranges and needn't reach their ends.
Inputs may be any that keep to these rules, and one draw needn't show every extreme that they name: `expert_ids`: each token names 8 different experts. Within the tokens of one index of expert (aligned blocks of 128 tokens) no expert is named more than 24 times, a bound that some block reaches.
All inputs are finite; a program needn't handle non-finite values.
Results may differ from the reference program's by a relative error of at most 0.015.
Values may be sent and summed in bfloat16 or wider, within the bound.
A program may use at most 128 MiB of HBM per device.

```python
import math
import jax
import jax.numpy as jnp
import numpy as np
from jax import lax

D = 4096
FF = 1536
TOPK = 8
TOK_DEV = 128
EXPERTS = 64
CAP = 24
SLOTS = 768
TOKENS = 4096
N_SECTION = 8
N_EXPERT = 32


def steps_of(rng, shape, cuts, smallest, largest):
    gain = 1.0
    for dim, parts in cuts:
        heights = jax.random.uniform(jax.random.fold_in(jax.random.fold_in(rng, 6), dim), (parts,), jnp.float32, smallest / len(cuts), largest / len(cuts))
        gain = gain * jnp.repeat(jnp.exp(heights), shape[dim] // parts).reshape((-1,) + (1,) * (len(shape) - 1 - dim))
    return gain


def shared_out(key, own, number, rows, number_of, top, most, lean):
    order = jax.random.permutation(key, number_of)
    heavy_load, usual = shares(number_of, rows * top, most, lean, True), shares(number_of, rows * top, most, lean, False)
    places = jnp.arange(number_of)

    def named(tallies, turn):
        used = int((tallies > 0).sum())
        fixed = max(1, used // 4)
        moved = fixed + (places - fixed + turn * (used - fixed)) % max(1, number_of - fixed)
        return jnp.zeros((number_of,), jnp.int32).at[order[jnp.where(places < fixed, places, moved)]].set(jnp.asarray(tallies, jnp.int32))

    tallies = jnp.where(number % 4 == 0, named(heavy_load, number // 4), named(usual, number - number // 4 - 1))
    mixed = jax.random.permutation(jax.random.fold_in(own, 3), number_of)
    giver, taker = mixed[0:number_of // 2 * 2:2], mixed[1:number_of // 2 * 2:2]
    slack = jnp.minimum(tallies[giver] - 1, most - tallies[taker]) // 2
    slack = jnp.where((giver == order[0]) | (taker == order[0]) | (tallies[taker] == 0), 0, jnp.maximum(slack, 0))
    moved = jax.random.randint(jax.random.fold_in(own, 4), (number_of // 2,), 0, 1 << 20) % (slack + 1)
    tallies = tallies.at[giver].add(-moved).at[taker].add(moved)
    members = jnp.searchsorted(jnp.cumsum(tallies), jnp.arange(rows * top), side="right").astype(jnp.int32)
    table = members.reshape(top, rows).T
    table = table[jax.random.permutation(jax.random.fold_in(own, 1), rows)]
    turn = jax.random.randint(jax.random.fold_in(own, 2), (rows, 1), 0, top)
    return jnp.take_along_axis(table, (jnp.arange(top)[None, :] + turn) % top, axis=1)


def shares(amount, total, most, skew, full):
    portions = [(1 << 20) // math.isqrt(grade ** skew) + 1 for grade in range(1, amount + 1)]
    largest = most if full else min(most, max(-(-total // amount), total * portions[0] // sum(portions)))
    least = 1 if total - largest >= amount - 1 else 0
    given, spare = [largest] + [least] * (amount - 1), total - largest - least * (amount - 1)
    while spare > 0:
        movable = [i for i in range(1, amount) if given[i] < largest] or [i for i in range(1, amount) if given[i] < most]
        whole, left = sum([portions[i] for i in movable]), spare
        for i in movable:
            extra = min(most - given[i], max(1, left * portions[i] // whole), spare)
            given[i] = given[i] + extra
            spare = spare - extra
    return np.array(given)


def noise(key, extent, scale, limit, shards=(), kind=jnp.bfloat16):
    level = steps_of(key, extent, shards, -0.22, 0.18) if shards else 1.0
    result = jax.random.normal(key, extent, jnp.float32) * scale * level
    return jnp.minimum(jnp.maximum(result, -limit), limit).astype(kind)


def setup_inputs(seed: int = 0) -> dict:
    arg_keys = jax.random.split(jax.random.key(seed), 9)
    grad_out = noise(arg_keys[0], (TOKENS, D), 1.0, 6.0, ((0, 32), (1, 8)))
    probs = jnp.clip(0.05 + 0.35 * jax.random.uniform(arg_keys[1], (TOKENS, TOPK), jnp.float32) ** steps_of(arg_keys[1], (TOKENS, TOPK), ((0, 32),), -0.2, 0.2), 0.05, 0.4)
    expert_ids_keys = jax.random.split(jax.random.fold_in(arg_keys[2], 1), TOKENS // TOK_DEV)
    expert_ids_turns = jax.random.permutation(jax.random.fold_in(arg_keys[2], 3), TOKENS // TOK_DEV)
    expert_ids = jax.vmap(lambda own, number: shared_out(jax.random.fold_in(arg_keys[2], 2), own, number, TOK_DEV, EXPERTS, TOPK, CAP, 2))(expert_ids_keys, expert_ids_turns).reshape((TOKENS, TOPK))
    w_gate = noise(arg_keys[3], (EXPERTS, FF, D), D ** -0.5, 0.09375, ((0, 32), (1, 8)))
    w_up = noise(arg_keys[4], (EXPERTS, FF, D), D ** -0.5, 0.09375, ((0, 32), (1, 8)))
    w_down = noise(arg_keys[5], (EXPERTS, FF, D), FF ** -0.5, 0.15625, ((0, 32), (1, 8)))
    saved_gate = noise(arg_keys[6], (EXPERTS, FF, SLOTS), 0.5, 3.0, ((0, 32), (1, 8)))
    saved_up = noise(arg_keys[7], (EXPERTS, FF, SLOTS), 0.5, 3.0, ((0, 32), (1, 8)))
    return dict(grad_out=grad_out, probs=probs, expert_ids=expert_ids, w_gate=w_gate, w_up=w_up, w_down=w_down, saved_gate=saved_gate, saved_up=saved_up)


def slot_index(expert_ids):
    blocks = expert_ids.reshape(N_EXPERT, TOK_DEV * TOPK)
    onehot = (blocks[:, :, None] == jnp.arange(EXPERTS, dtype=jnp.int32)[None, None, :]).astype(jnp.int32)
    before = jnp.cumsum(onehot, axis=1) - onehot
    position = jnp.sum(before * onehot, axis=2).astype(jnp.int32)
    source = jnp.arange(N_EXPERT, dtype=jnp.int32)[:, None]
    flat = blocks * SLOTS + source * CAP + position
    return flat.reshape(-1).astype(jnp.int32)


def reference(grad_out, probs, expert_ids, w_gate, w_up, w_down, saved_gate, saved_up):
    flat = slot_index(expert_ids)
    owner = (jnp.arange(TOKENS * TOPK, dtype=jnp.int32) // TOPK).astype(jnp.int32)
    table = jnp.full((EXPERTS * SLOTS,), TOKENS, jnp.int32).at[flat].set(owner)
    padded = jnp.concatenate([grad_out, jnp.zeros((1, D), jnp.bfloat16)], axis=0)
    group = FF // N_SECTION

    def expert_step(item):
        table_row, gate_rows, up_rows, down_rows, gate_saved, up_saved = item
        dispatched = padded[table_row]
        hidden_grad = jnp.dot(dispatched, down_rows.T, preferred_element_type=jnp.float32)
        gate_act = gate_saved.astype(jnp.float32).T
        up_act = up_saved.astype(jnp.float32).T
        sigmoid_gate = jax.nn.sigmoid(gate_act)
        silu_gate = gate_act * sigmoid_gate
        router = jnp.sum(silu_gate * up_act * hidden_grad, axis=1).astype(jnp.bfloat16)
        gate_grad = (hidden_grad * up_act * sigmoid_gate * (1.0 + gate_act * (1.0 - sigmoid_gate))).astype(jnp.bfloat16)
        up_grad = (hidden_grad * silu_gate).astype(jnp.bfloat16)
        gate_parts = gate_grad.astype(jnp.float32).reshape(SLOTS, N_SECTION, group)
        up_parts = up_grad.astype(jnp.float32).reshape(SLOTS, N_SECTION, group)
        gate_mat = gate_rows.astype(jnp.float32).reshape(N_SECTION, group, D)
        up_mat = up_rows.astype(jnp.float32).reshape(N_SECTION, group, D)
        partial_value = jnp.einsum('srf,rfd->rsd', gate_parts, gate_mat) + jnp.einsum('srf,rfd->rsd', up_parts, up_mat)
        rounded = lax.optimization_barrier(partial_value.astype(jnp.bfloat16))
        expert_grad = jnp.sum(rounded.astype(jnp.float32), axis=0).astype(jnp.bfloat16)
        return expert_grad, router

    expert_grad, router_grad = lax.map(expert_step, (table.reshape(EXPERTS, SLOTS), w_gate, w_up, w_down, saved_gate, saved_up))
    picked = expert_grad.reshape(EXPERTS * SLOTS, D)[flat].reshape(TOKENS, TOPK, D)
    grad_in = jnp.sum(picked.astype(jnp.float32) * probs[:, :, None], axis=1).astype(jnp.bfloat16)
    grad_probs = router_grad.reshape(-1)[flat].reshape(TOKENS, TOPK)
    return grad_in, grad_probs
```

```python
import jax
import jax.numpy as jnp
from jax import lax
from jax.experimental import pallas as pl
from jax.experimental.pallas import tpu as pltpu
from jax.sharding import PartitionSpec as P

TOPK = 8
NZ = 8
CAP = 24
TB = 128
MESH = pl.DeviceIdType.MESH
F32 = jnp.float32
BF16 = jnp.bfloat16


def kernel(
    ids_ref, probs_ref, x_hbm, wg_hbm, wu_hbm, wd_hbm, sg_hbm, su_hbm,
    out_ref, gp_ref,
    tok, wg, wu, wd, sg, su, down, dpar, sendbuf, part, rbuf, fin, back,
    idsall, masks, codes, rown, rrecv, rcol, whi, wlo, onehot, ggs, ugs,
    ld_sem, x_sem, zs_sem, zr_sem, ids_s, ids_r, st1_s, fw1_s, st2_s, fw2_s, tok_r,
    dp_s, dp_r, rs_s, rs_r, rt_s, rt_r, bk_s, bk_r,
):
    z = lax.axis_index("section")
    e = lax.axis_index("expert")
    x, y, c = e // 8, (e // 2) % 4, e % 2
    partner = e + 1 - 2 * c
    zp, zm = (z + 1) % NZ, (z + NZ - 1) % NZ
    D = tok.shape[2]
    DS = D // NZ
    F = wd.shape[1]

    def dev(cc, i, j):
        ax = (x * (1 - cc) + y * cc + i) % 4
        ay = (y * (1 - cc) + x * cc + j) % 4
        return ((ax * (1 - cc) + ay * cc) * 4 + (ay * (1 - cc) + ax * cc)) * 2 + cc

    def gray(m):
        return m + (m // 2) * (1 - 2 * (m % 2))

    def place(k, m):
        mid = (k * (3 - k)) // 2
        v = 2 * ((k + 2) % 3) + m // 2
        i = gray(m) * (1 - mid) + gray(v) * mid
        j = 2 * (k // 3) * (1 - mid) + (1 + 2 * (m % 2)) * mid
        return i, j

    def rcopy(src, dst, ssem, rsem, zz, ee):
        return pltpu.make_async_remote_copy(
            src_ref=src, dst_ref=dst, send_sem=ssem, recv_sem=rsem,
            device_id=(zz, ee), device_id_type=MESH,
        )

    def cols(q):
        return pl.ds(pl.multiple_of(q * DS, DS), DS)

    xcopy = pltpu.make_async_copy(x_hbm, tok.at[0, :, cols(z)], x_sem)
    xcopy.start()
    loads = [
        pltpu.make_async_copy(a, b, ld_sem.at[n])
        for n, (a, b) in enumerate(
            ((sg_hbm, sg), (su_hbm, su), (wd_hbm, wd), (wg_hbm, wg), (wu_hbm, wu))
        )
    ]
    idcopy = pltpu.make_async_copy(ids_ref, idsall.at[0], ld_sem.at[5])
    idcopy.start()

    barrier = pltpu.get_barrier_semaphore()

    def greet_z(n, carry):
        pl.semaphore_signal(barrier, inc=1, device_id=((z + n) % NZ, e), device_id_type=MESH)
        return carry

    def greet_e(n, carry):
        pl.semaphore_signal(barrier, inc=1, device_id=(z, (e + n) % 32), device_id_type=MESH)
        return carry

    lax.fori_loop(1, NZ, greet_z, 0)
    lax.fori_loop(1, 32, greet_e, 0)
    pl.semaphore_wait(barrier, NZ - 1 + 31)

    xcopy.wait()
    idcopy.wait()

    a1p, a1m = dev(c, 1, 0), dev(c, 3, 0)
    a2p, a2m = dev(c, 0, 1), dev(c, 0, 3)
    half = TB // 2

    def zpiece(q, rows):
        return tok.at[0, rows, cols(q)]

    full, lo, hi = pl.ds(0, TB), pl.ds(0, half), pl.ds(half, half)

    def zsend(d, s):
        q = (z + NZ - s) % NZ if d == 0 else (z + s) % NZ
        rows = full if s < 3 else (lo if d == 0 else hi)
        return rcopy(
            zpiece(q, rows), zpiece(q, rows), zs_sem.at[d, s], zr_sem.at[d, s],
            zp if d == 0 else zm, e,
        )

    def zrecv(d, s):
        q = (z + NZ - 1 - s) % NZ if d == 0 else (z + 1 + s) % NZ
        rows = full if s < 3 else (lo if d == 0 else hi)
        return rcopy(
            zpiece(q, rows), zpiece(q, rows), zs_sem.at[d, s], zr_sem.at[d, s],
            zp if d == 0 else zm, e,
        )

    def first(q):
        rcopy(tok.at[0, :, cols(q)], tok.at[2, :, cols(q)], st1_s.at[0], tok_r.at[2, 0], z, a1p).start()
        rcopy(tok.at[0, :, cols(q)], tok.at[1, :, cols(q)], st1_s.at[1], tok_r.at[1, 0], z, a1m).start()

    zsend(0, 0).start()
    zsend(1, 0).start()

    def send_ids(n, carry):
        i, j = n // 4, n % 4
        mi, jj = gray((4 - i) % 4), (4 - j) % 4
        odd = jj % 2
        slot = (1 - odd) * (6 * jj + mi) + odd * (4 + 2 * mi + jj // 2)
        rcopy(idsall.at[0], idsall.at[slot], ids_s, ids_r, z, dev(c, i, j)).start()
        return carry

    lax.fori_loop(1, 16, send_ids, 0)
    first(z)
    for cp in loads:
        cp.start()
    for s in range(1, 4):
        zrecv(0, s - 1).wait_recv()
        zsend(0, s).start()
        zrecv(1, s - 1).wait_recv()
        zsend(1, s).start()
        first((z + NZ - s) % NZ)
        first((z + s) % NZ)
    zrecv(0, 3).wait_recv()
    zrecv(1, 3).wait_recv()
    first((z + 4) % NZ)

    rcopy(idsall.at[1:16], idsall.at[1:16], ids_s, ids_r, z, a1p).wait_recv()
    row8 = lax.broadcasted_iota(jnp.int32, (8, TB), 0)
    mine = jnp.where(row8 < 2, 2 * e + row8, 2 * partner + row8 - 2)
    mine = jnp.where(row8 < 4, mine, -1)

    def mask_of(n, carry):
        table = idsall[n]
        hit = jnp.zeros((8, TB), F32)
        for k in range(TOPK):
            hit = hit + jnp.where(table[k : k + 1, :] == mine, 1.0, 0.0)
        masks[n] = hit
        return carry

    lax.fori_loop(0, 16, mask_of, 0)
    r128 = lax.broadcasted_iota(jnp.int32, (TB, TB), 0)
    l128 = lax.broadcasted_iota(jnp.int32, (TB, TB), 1)
    tri = jnp.where(r128 < l128, 1.0, 0.0).astype(BF16)
    mk = masks[...].reshape(TB, TB)
    ps = jnp.dot(mk.astype(BF16), tri, preferred_element_type=F32)
    codes[...] = jnp.where(mk > 0.5, ps, -1.0).reshape(16, 8, TB)

    hit = jnp.zeros((TB, TB), F32)
    pe = jnp.zeros((TB, TB), F32)
    for k in range(TOPK):
        same = ids_ref[k : k + 1, :] == r128
        hit = hit + jnp.where(same, 1.0, 0.0)
        pe = pe + jnp.where(same, probs_ref[k : k + 1, :], 0.0)
    ps = jnp.dot(hit.astype(BF16), tri, preferred_element_type=F32)
    code_te = jnp.where(hit > 0.5, ps, -1.0).T.astype(BF16)
    prob_te = pe.T
    prob_hi = prob_te.astype(BF16)
    prob_lo = (prob_te - prob_hi.astype(F32)).astype(BF16)
    LT = onehot.shape[1]
    for lt in range(0, LT, 512):
        el = lax.broadcasted_iota(jnp.int32, (TB, 512), 0)
        ll = lax.broadcasted_iota(jnp.int32, (TB, 512), 1) + lt
        off = ll - CAP * el
        spread = jnp.where((off >= 0) & (off < CAP), 1.0, 0.0)
        s_of = jnp.sum(spread * off.astype(F32), axis=0, keepdims=True)
        spread = spread.astype(BF16)
        code_l = jnp.dot(code_te, spread, preferred_element_type=F32)
        prob_l = jnp.dot(prob_hi, spread, preferred_element_type=F32) + jnp.dot(
            prob_lo, spread, preferred_element_type=F32
        )
        oh = jnp.where(jnp.abs(code_l - s_of) < 0.5, 1.0, 0.0)
        w = oh * prob_l
        w_hi = w.astype(BF16)
        onehot[:, lt : lt + 512] = oh.astype(BF16)
        whi[:, lt : lt + 512] = w_hi
        wlo[:, lt : lt + 512] = (w - w_hi.astype(F32)).astype(BF16)

    def second(mi):
        rcopy(tok.at[mi], tok.at[5 + 2 * mi], st2_s.at[mi, 0], tok_r.at[5 + 2 * mi, 0], z, a2p).start()
        rcopy(tok.at[mi], tok.at[4 + 2 * mi], st2_s.at[mi, 1], tok_r.at[4 + 2 * mi, 0], z, a2m).start()

    def whole(n):
        return rcopy(tok.at[n], tok.at[n], st2_s.at[0, 0], tok_r.at[n, 0], z, a2p)

    def half_of(n, h):
        rows = pl.ds(h * half, half)
        return rcopy(tok.at[n, rows], tok.at[n, rows], st2_s.at[0, 0], tok_r.at[n, h], z, a2p)

    fwd1_hi = rcopy(tok.at[1, hi], tok.at[3, hi], fw1_s.at[1], tok_r.at[3, 1], z, a1m)
    fwd1_lo = rcopy(tok.at[2, lo], tok.at[3, lo], fw1_s.at[0], tok_r.at[3, 0], z, a1p)
    whole(1).wait_recv()
    fwd1_hi.start()
    whole(2).wait_recv()
    fwd1_lo.start()
    second(0)
    second(1)
    second(2)
    for cp in loads:
        cp.wait()

    def arrive(it, m):
        @pl.when((it >= 1) & (it <= 2))
        def _():
            n = 4 * it + m
            u = 4 * (it - 1) + m
            whole(n).wait_recv()
            jj = m % 2
            rows = pl.ds((1 - jj) * half, half)
            n2 = 12 + u // 2
            rcopy(
                tok.at[n, rows], tok.at[n2, rows], fw2_s.at[u], tok_r.at[n2, 1 - jj],
                z, a2p if jj == 1 else a2m,
            ).start()

        @pl.when(it == 3)
        def _():
            half_of(12 + m, 0).wait_recv()
            half_of(12 + m, 1).wait_recv()

    s24 = lax.broadcasted_iota(jnp.int32, (CAP, TB), 0).astype(F32)

    def dsend(k, pair, ee):
        return rcopy(
            sendbuf.at[pair, ee], dpar.at[k, ee, pair], dp_s.at[pair, ee], dp_r.at[k, ee, pair],
            z, partner,
        )

    def dispatch(it, pair):
        n0 = 4 * it + 2 * pair
        code0, code1 = codes[n0], codes[n0 + 1]
        zero = jnp.zeros((CAP, TB), F32)
        blocks = []
        for q in range(4):
            b0 = jnp.where(jnp.abs(code0[q : q + 1, :] - s24) < 0.5, 1.0, 0.0)
            b1 = jnp.where(jnp.abs(code1[q : q + 1, :] - s24) < 0.5, 1.0, 0.0)
            blocks.append(jnp.concatenate([b0, zero], axis=1))
            blocks.append(jnp.concatenate([zero, b1], axis=1))
        pick = jnp.concatenate(blocks, axis=0).astype(BF16)

        @pl.when(it >= 1)
        def _():
            dsend(it - 1, pair, 0).wait_send()
            dsend(it - 1, pair, 1).wait_send()

        def tile(t, carry):
            cs = pl.ds(pl.multiple_of(t * 512, 512), 512)
            rows = tok[pl.ds(n0, 2), :, cs].reshape(2 * TB, 512)
            got = jnp.dot(pick, rows, preferred_element_type=F32).astype(BF16)
            down[0, pair, :, cs] = got[0:48]
            down[1, pair, :, cs] = got[48:96]
            sendbuf[pair, 0, :, cs] = got[96:144]
            sendbuf[pair, 1, :, cs] = got[144:192]
            return carry

        lax.fori_loop(0, D // 512, tile, 0)
        dsend(it, pair, 0).start()
        dsend(it, pair, 1).start()

    NT = (((1,), (1,)), ((), ()))

    def saved_rows(it):
        base = lax.broadcasted_iota(jnp.int32, (CAP, sg.shape[2]), 1) - lax.broadcasted_iota(
            jnp.int32, (CAP, sg.shape[2]), 0
        )
        blocks = []
        for o in range(2):
            cc = c if o == 0 else 1 - c
            for m in range(4):
                i, j = place(it, m)
                blocks.append(jnp.where(base == dev(cc, i, j) * CAP, 1.0, 0.0))
        return jnp.concatenate(blocks, axis=0).astype(BF16)

    def hidden(it, ee, perm, eye):
        acc = jnp.zeros((192, F), F32)
        for kt in range(0, D, 512):
            rows = jnp.concatenate(
                [
                    down[ee, :, :, kt : kt + 512].reshape(96, 512),
                    dpar[it, ee, :, :, kt : kt + 512].reshape(96, 512),
                ],
                axis=0,
            )
            acc = acc + lax.dot_general(
                rows, wd[ee, :, kt : kt + 512], NT, preferred_element_type=F32
            )
        g = lax.dot_general(perm, sg[ee], NT, preferred_element_type=F32)
        u = lax.dot_general(perm, su[ee], NT, preferred_element_type=F32)
        s = 1.0 / (1.0 + jnp.exp(-g))
        silu = g * s
        router = jnp.sum(silu * u * acc, axis=1, keepdims=True)
        rown[it, ee : ee + 1, 0:192] = jnp.sum(router * eye, axis=0, keepdims=True)
        ggs[ee] = (acc * u * s * (1.0 + g * (1.0 - s))).astype(BF16)
        ugs[ee] = (acc * silu).astype(BF16)

    def eye_of():
        return jnp.where(
            lax.broadcasted_iota(jnp.int32, (192, 192), 0)
            == lax.broadcasted_iota(jnp.int32, (192, 192), 1),
            1.0,
            0.0,
        )

    def rs_wait_send(buf, ee):
        rcopy(
            part.at[buf, ee, 0:7], part.at[buf, ee, 0:7], rs_s.at[buf, ee], rs_r.at[0, 0, ee, 0],
            zp, e,
        ).wait_send()

    def partial(it, ee):
        buf = it % 2

        @pl.when(it >= 2)
        def _():
            rs_wait_send(buf, ee)

        gg, ug = ggs[ee], ugs[ee]

        def tile(t, carry):
            cs = cols(t)
            v = jnp.dot(gg, wg[ee, :, cs], preferred_element_type=F32) + jnp.dot(
                ug, wu[ee, :, cs], preferred_element_type=F32
            )
            part[buf, ee, t] = v.astype(BF16).reshape(4, 48, DS)
            return carry

        lax.fori_loop(0, NZ, tile, 0)

    def router_copy(k, n):
        return rcopy(rown.at[k], rrecv.at[k, n - 1], rt_s.at[k], rt_r.at[k], (z + n) % NZ, e)

    def send_router(it):
        def go(n, carry):
            router_copy(it, n).start()
            return carry

        lax.fori_loop(1, NZ, go, 0)

    def work(it, s):
        if s == 0:
            arrive(it, 0)
            arrive(it, 1)
            dispatch(it, 0)
        elif s == 1:
            arrive(it, 2)
        elif s == 2:
            @pl.when(it == 0)
            def _():
                half_of(3, 0).wait_recv()
                half_of(3, 1).wait_recv()
                second(3)

            arrive(it, 3)
            dispatch(it, 1)
        elif s == 3:
            for ee in range(2):
                for pair in range(2):
                    dsend(it, pair, ee).wait_recv()
            hidden(it, 0, saved_rows(it), eye_of())
        elif s == 4:
            hidden(it, 1, saved_rows(it), eye_of())
            send_router(it)
        elif s == 5:
            partial(it, 0)
        else:
            partial(it, 1)

    def rs_copy(k, s, ee, sub):
        t = (z + 2 * NZ - 1 - s) % NZ if ee == 0 else (z + 1 + s) % NZ
        return rcopy(
            part.at[k % 2, ee, t, sub], rbuf.at[k, s, ee, sub], rs_s.at[k % 2, ee],
            rs_r.at[k, s, ee, sub], zp if ee == 0 else zm, e,
        ), t

    def ring(k, s):
        def one(sub, carry):
            for ee in range(2):
                cp, t = rs_copy(k, s, ee, sub)
                if s:
                    rs_copy(k, s - 1, ee, sub)[0].wait_recv()
                    part[k % 2, ee, t, sub] = (
                        part[k % 2, ee, t, sub].astype(F32)
                        + rbuf[k, s - 1, ee, sub].astype(F32)
                    ).astype(BF16)
                cp.start()
            return carry

        lax.fori_loop(0, 4, one, 0)

    def message(n, cc, i, j):
        return rcopy(fin.at[n], back.at[e], bk_s, bk_r, z, dev(cc, i, j))

    def finish(k):
        rcopy(rrecv.at[k], rrecv.at[k], rt_s.at[k], rt_r.at[k], zp, e).wait()
        rows = rown[k]
        for n in range(NZ - 1):
            rows = rows + rrecv[k, n]
        eye = eye_of()
        for ee in range(2):
            col = jnp.sum(rows[ee : ee + 1, 0:192] * eye, axis=1, keepdims=True)
            rcol[ee] = jnp.broadcast_to(col, (192, 128)).reshape(4, 48, 128)

        def one(sub, carry):
            got = []
            for ee in range(2):
                rs_copy(k, NZ - 2, ee, sub)[0].wait_recv()
                got.append(
                    part[k % 2, ee, z, sub].astype(F32) + rbuf[k, NZ - 2, ee, sub].astype(F32)
                )
            o, pair = sub // 2, sub % 2
            cc = c * (1 - o) + (1 - c) * o
            for a in range(2):
                n = 8 * k + 2 * sub + a
                sl = slice(24 * a, 24 * a + 24)
                fin[n, :, 0:DS] = jnp.concatenate([got[0][sl], got[1][sl]], axis=0).astype(BF16)
                fin[n, :, DS : DS + 128] = jnp.concatenate(
                    [rcol[0, sub, sl], rcol[1, sub, sl]], axis=0
                ).astype(BF16)
                i, j = place(k, 2 * pair + a)
                if a == 0:
                    own = (k == 0) & (sub == 0)

                    @pl.when(own)
                    def _():
                        back[e] = fin[n]

                    @pl.when(jnp.logical_not(own))
                    def _():
                        message(n, cc, i, j).start()
                else:
                    message(n, cc, i, j).start()
            return carry

        lax.fori_loop(0, 4, one, 0)

    def step(it, carry):
        for s in range(7):
            @pl.when((it >= 1) & (it <= 4))
            def _():
                ring(it - 1, s)

            if s == 0:
                @pl.when(it >= 2)
                def _():
                    finish(it - 2)

            @pl.when(it <= 3)
            def _():
                work(it, s)

        return carry

    lax.fori_loop(0, 6, step, 0)

    rcopy(back.at[0:31], back.at[0:31], bk_s, bk_r, z, partner).wait()
    rows = back[:, :, 0:DS].reshape(LT, DS)
    out_ref[...] = (
        jnp.dot(whi[...], rows, preferred_element_type=F32)
        + jnp.dot(wlo[...], rows, preferred_element_type=F32)
    ).astype(BF16)
    off = lax.broadcasted_iota(jnp.int32, (LT, 128), 0) - CAP * lax.broadcasted_iota(
        jnp.int32, (LT, 128), 1
    )
    route = back[:, :, DS : DS + 128].reshape(LT, 128).astype(F32)
    route = jnp.where((off >= 0) & (off < CAP), route, 0.0).astype(BF16)
    vt = jnp.dot(onehot[...], route, preferred_element_type=F32).T
    for k in range(TOPK):
        gp_ref[k : k + 1, :] = jnp.sum(
            jnp.where(ids_ref[k : k + 1, :] == r128, vt, 0.0), axis=0, keepdims=True
        )

    for d in range(2):
        for s in range(4):
            zsend(d, s).wait_send()
    rcopy(idsall.at[1:16], idsall.at[1:16], ids_s, ids_r, z, a1p).wait_send()
    for d in range(2):
        rcopy(tok.at[0], tok.at[1], st1_s.at[d], tok_r.at[1, 0], z, a1p).wait_send()
    fwd1_hi.wait_send()
    fwd1_lo.wait_send()
    for mi in range(4):
        for d in range(2):
            rcopy(tok.at[mi], tok.at[5], st2_s.at[mi, d], tok_r.at[5, 0], z, a2p).wait_send()
    for u in range(8):
        rcopy(tok.at[4, lo], tok.at[12, lo], fw2_s.at[u], tok_r.at[12, 0], z, a2p).wait_send()
    for pair in range(2):
        for ee in range(2):
            dsend(3, pair, ee).wait_send()
    for buf in range(2):
        for ee in range(2):
            rs_wait_send(buf, ee)


def local(grad_out, probs, expert_ids, w_gate, w_up, w_down, saved_gate, saved_up):
    D, F, S = w_gate.shape[2], w_gate.shape[1], saved_gate.shape[2]
    DS = D // NZ
    vm = pl.BlockSpec(memory_space=pltpu.VMEM)
    hbm = pl.BlockSpec(memory_space=pl.ANY)
    dma = pltpu.SemaphoreType.DMA
    out, gp = pl.pallas_call(
        kernel,
        out_shape=(
            jax.ShapeDtypeStruct((TB, DS), BF16),
            jax.ShapeDtypeStruct((TOPK, TB), F32),
        ),
        in_specs=[vm, vm] + [hbm] * 6,
        out_specs=(vm, vm),
        scratch_shapes=[
            pltpu.VMEM((16, TB, D), BF16),
            pltpu.VMEM((2, F, D), BF16),
            pltpu.VMEM((2, F, D), BF16),
            pltpu.VMEM((2, F, D), BF16),
            pltpu.VMEM((2, F, S), BF16),
            pltpu.VMEM((2, F, S), BF16),
            pltpu.VMEM((2, 2, 48, D), BF16),
            pltpu.VMEM((4, 2, 2, 48, D), BF16),
            pltpu.VMEM((2, 2, 48, D), BF16),
            pltpu.VMEM((2, 2, NZ, 4, 48, DS), BF16),
            pltpu.VMEM((4, NZ - 1, 2, 4, 48, DS), BF16),
            pltpu.VMEM((32, 48, DS + 128), BF16),
            pltpu.VMEM((32, 48, DS + 128), BF16),
            pltpu.VMEM((16, TOPK, TB), jnp.int32),
            pltpu.VMEM((16, 8, TB), F32),
            pltpu.VMEM((16, 8, TB), F32),
            pltpu.VMEM((4, 8, 256), F32),
            pltpu.VMEM((4, NZ - 1, 8, 256), F32),
            pltpu.VMEM((2, 4, 48, 128), F32),
            pltpu.VMEM((TB, 1536), BF16),
            pltpu.VMEM((TB, 1536), BF16),
            pltpu.VMEM((TB, 1536), BF16),
            pltpu.VMEM((2, 192, F), BF16),
            pltpu.VMEM((2, 192, F), BF16),
            dma((6,)),
            dma,
            dma((2, 4)),
            dma((2, 4)),
            dma,
            dma,
            dma((2,)),
            dma((2,)),
            dma((4, 2)),
            dma((8,)),
            dma((16, 2)),
            dma((2, 2)),
            dma((4, 2, 2)),
            dma((2, 2)),
            dma((4, NZ - 1, 2, 4)),
            dma((4,)),
            dma((4,)),
            dma,
            dma,
        ],
        compiler_params=pltpu.CompilerParams(
            collective_id=0, has_side_effects=True, vmem_limit_bytes=67043328
        ),
    )(expert_ids.T, probs.T, grad_out, w_gate, w_up, w_down, saved_gate, saved_up)
    return out, gp.astype(BF16).T


def solution(mesh):
    placed = (
        P("expert", "section"),
        P("expert", None),
        P("expert", None),
        P("expert", "section", None),
        P("expert", "section", None),
        P("expert", "section", None),
        P("expert", "section", None),
        P("expert", "section", None),
    )
    return jax.shard_map(
        local,
        mesh=mesh,
        in_specs=placed,
        out_specs=(P("expert", "section"), P("expert", None)),
        check_vma=False,
    )
```

```python
import jax
import jax.numpy as jnp
from jax import lax
from jax.experimental import pallas as pl
from jax.experimental.pallas import tpu as pltpu
from jax.sharding import PartitionSpec as P

TOPK = 8
NZ = 8
CAP = 24
TB = 128
MESH = pl.DeviceIdType.MESH
F32 = jnp.float32
BF16 = jnp.bfloat16


def kernel(
    ids_ref, probs_ref, x_hbm, wg_hbm, wu_hbm, wd_hbm, sg_hbm, su_hbm,
    out_ref, gp_ref,
    tok, wgu, wd, sg, su, down, dpar, sendbuf, part, rbuf, fin, back,
    idsall, masks, codes, rown, rrecv, rcol, whi, wlo, onehot, gus,
    ld_sem, x_sem, zs_sem, zr_sem, ids_s, ids_r, st1_s, fw1_s, st2_s, fw2_s, tok_r,
    dp_s, dp_r, rs_s, rs_r, rt_s, rt_r, bk_s, bk_r,
):
    z = lax.axis_index("section")
    e = lax.axis_index("expert")
    x, y, c = e // 8, (e // 2) % 4, e % 2
    partner = e + 1 - 2 * c
    zp, zm = (z + 1) % NZ, (z + NZ - 1) % NZ
    D = tok.shape[2]
    DS = D // NZ
    F = wd.shape[1]

    def dev(cc, i, j):
        ax = (x * (1 - cc) + y * cc + i) % 4
        ay = (y * (1 - cc) + x * cc + j) % 4
        return ((ax * (1 - cc) + ay * cc) * 4 + (ay * (1 - cc) + ax * cc)) * 2 + cc

    def gray(m):
        return m + (m // 2) * (1 - 2 * (m % 2))

    def place(n):
        k, m = n // 4, n % 4
        mid = (k * (3 - k)) // 2
        v = 2 * ((k + 2) % 3) + m // 2
        i = gray(m) * (1 - mid) + gray(v) * mid
        j = 2 * (k // 3) * (1 - mid) + (1 + 2 * (m % 2)) * mid
        return i, j

    def rcopy(src, dst, ssem, rsem, zz, ee):
        return pltpu.make_async_remote_copy(
            src_ref=src, dst_ref=dst, send_sem=ssem, recv_sem=rsem,
            device_id=(zz, ee), device_id_type=MESH,
        )

    def cols(q):
        return pl.ds(pl.multiple_of(q * DS, DS), DS)

    xcopy = pltpu.make_async_copy(x_hbm, tok.at[0, :, cols(z)], x_sem)
    xcopy.start()
    loads = [
        pltpu.make_async_copy(a, b, ld_sem.at[n])
        for n, (a, b) in enumerate(
            ((sg_hbm, sg), (su_hbm, su), (wd_hbm, wd), (wg_hbm, wgu.at[:, 0:F]), (wu_hbm, wgu.at[:, F : 2 * F]))
        )
    ]
    idcopy = pltpu.make_async_copy(ids_ref, idsall.at[0], ld_sem.at[5])
    idcopy.start()

    barrier = pltpu.get_barrier_semaphore()

    def greet_z(n, carry):
        pl.semaphore_signal(barrier, inc=1, device_id=((z + n) % NZ, e), device_id_type=MESH)
        return carry

    def greet_e(n, carry):
        pl.semaphore_signal(barrier, inc=1, device_id=(z, (e + n) % 32), device_id_type=MESH)
        return carry

    lax.fori_loop(1, NZ, greet_z, 0)
    lax.fori_loop(1, 32, greet_e, 0)
    pl.semaphore_wait(barrier, NZ - 1 + 31)

    xcopy.wait()
    idcopy.wait()

    a1p, a1m = dev(c, 1, 0), dev(c, 3, 0)
    a2p, a2m = dev(c, 0, 1), dev(c, 0, 3)
    half = TB // 2

    lo, hi = pl.ds(0, half), pl.ds(half, half)

    def zhalf(q, d, s, h):
        rows = pl.ds(h * half, half)
        return rcopy(
            tok.at[0, rows, cols(q)], tok.at[0, rows, cols(q)], zs_sem.at[d, s, h],
            zr_sem.at[d, s, h], zp if d == 0 else zm, e,
        )

    def zsend(d, s, h):
        return zhalf((z + NZ - s) % NZ if d == 0 else (z + s) % NZ, d, s, h)

    def zrecv(d, s, h):
        return zhalf((z + NZ - 1 - s) % NZ if d == 0 else (z + 1 + s) % NZ, d, s, h)

    def first(q):
        for n, slot, ssem, to in (
            (0, 2, st1_s.at[0], a1p), (1, 1, st1_s.at[1], a1m),
            (2, 5, st2_s.at[0, 0], a2p), (3, 4, st2_s.at[0, 1], a2m),
        ):
            rcopy(tok.at[0, :, cols(q)], tok.at[slot, :, cols(q)], ssem, tok_r.at[slot, 0], z, to).start()

    for h in range(2):
        for d in range(2):
            zsend(d, 0, h).start()

    def send_ids(n, carry):
        i, j = n // 4, n % 4
        mi, jj = gray((4 - i) % 4), (4 - j) % 4
        odd = jj % 2
        slot = (1 - odd) * (6 * jj + mi) + odd * (4 + 2 * mi + jj // 2)
        rcopy(idsall.at[0], idsall.at[slot], ids_s, ids_r, z, dev(c, i, j)).start()
        return carry

    first(z)
    lax.fori_loop(1, 16, send_ids, 0)
    for cp in loads:
        cp.start()
    for s in range(1, 4):
        for h in range(2):
            for d in range(2):
                zrecv(d, s - 1, h).wait_recv()
                if s < 3 or h == d:
                    zsend(d, s, h).start()
        first((z + NZ - s) % NZ)
        first((z + s) % NZ)
    zrecv(0, 3, 0).wait_recv()
    zrecv(1, 3, 1).wait_recv()
    first((z + 4) % NZ)

    rcopy(idsall.at[1:16], idsall.at[1:16], ids_s, ids_r, z, a1p).wait_recv()
    row8 = lax.broadcasted_iota(jnp.int32, (8, TB), 0)
    mine = jnp.where(row8 < 2, 2 * e + row8, 2 * partner + row8 - 2)
    mine = jnp.where(row8 < 4, mine, -1)

    def mask_of(n, carry):
        table = idsall[n]
        hit = jnp.zeros((8, TB), F32)
        for k in range(TOPK):
            hit = hit + jnp.where(table[k : k + 1, :] == mine, 1.0, 0.0)
        masks[n] = hit
        return carry

    lax.fori_loop(0, 16, mask_of, 0)
    r128 = lax.broadcasted_iota(jnp.int32, (TB, TB), 0)
    l128 = lax.broadcasted_iota(jnp.int32, (TB, TB), 1)
    tri = jnp.where(r128 < l128, 1.0, 0.0).astype(BF16)
    mk = masks[...].reshape(TB, TB)
    ps = jnp.dot(mk.astype(BF16), tri, preferred_element_type=F32)
    codes[...] = jnp.where(mk > 0.5, ps, -1.0).reshape(16, 8, TB)

    LT = onehot.shape[1]

    def weights():
        hit = jnp.zeros((TB, TB), F32)
        pe = jnp.zeros((TB, TB), F32)
        for k in range(TOPK):
            same = ids_ref[k : k + 1, :] == r128
            hit = hit + jnp.where(same, 1.0, 0.0)
            pe = pe + jnp.where(same, probs_ref[k : k + 1, :], 0.0)
        ps = jnp.dot(hit.astype(BF16), tri, preferred_element_type=F32)
        code_te = jnp.where(hit > 0.5, ps, -1.0).T.astype(BF16)
        prob_te = pe.T
        prob_hi = prob_te.astype(BF16)
        prob_lo = (prob_te - prob_hi.astype(F32)).astype(BF16)
        for lt in range(0, LT, 512):
            el = lax.broadcasted_iota(jnp.int32, (TB, 512), 0)
            ll = lax.broadcasted_iota(jnp.int32, (TB, 512), 1) + lt
            off = ll - CAP * el
            spread = jnp.where((off >= 0) & (off < CAP), 1.0, 0.0)
            s_of = jnp.sum(spread * off.astype(F32), axis=0, keepdims=True)
            spread = spread.astype(BF16)
            code_l = jnp.dot(code_te, spread, preferred_element_type=F32)
            prob_l = jnp.dot(prob_hi, spread, preferred_element_type=F32) + jnp.dot(
                prob_lo, spread, preferred_element_type=F32
            )
            oh = jnp.where(jnp.abs(code_l - s_of) < 0.5, 1.0, 0.0)
            w = oh * prob_l
            w_hi = w.astype(BF16)
            onehot[:, lt : lt + 512] = oh.astype(BF16)
            whi[:, lt : lt + 512] = w_hi
            wlo[:, lt : lt + 512] = (w - w_hi.astype(F32)).astype(BF16)

    def second(mi):
        rcopy(tok.at[mi], tok.at[5 + 2 * mi], st2_s.at[mi, 0], tok_r.at[5 + 2 * mi, 0], z, a2p).start()
        rcopy(tok.at[mi], tok.at[4 + 2 * mi], st2_s.at[mi, 1], tok_r.at[4 + 2 * mi, 0], z, a2m).start()

    def whole(n):
        return rcopy(tok.at[n], tok.at[n], st2_s.at[0, 0], tok_r.at[n, 0], z, a2p)

    def half_of(n, h):
        rows = pl.ds(h * half, half)
        return rcopy(tok.at[n, rows], tok.at[n, rows], st2_s.at[0, 0], tok_r.at[n, h], z, a2p)

    fwd1_hi = rcopy(tok.at[1, hi], tok.at[3, hi], fw1_s.at[1], tok_r.at[3, 1], z, a1m)
    fwd1_lo = rcopy(tok.at[2, lo], tok.at[3, lo], fw1_s.at[0], tok_r.at[3, 0], z, a1p)
    whole(1).wait_recv()
    fwd1_hi.start()
    second(1)
    whole(2).wait_recv()
    fwd1_lo.start()
    second(2)
    for cp in loads:
        cp.wait()

    def arrive(it):
        @pl.when(it == 1)
        def _():
            half_of(3, 0).wait_recv()
            half_of(3, 1).wait_recv()
            second(3)

        @pl.when((it >= 2) & (it <= 5))
        def _():
            for a in range(2):
                n = 2 * it + a
                whole(n).wait_recv()
                rows = pl.ds((1 - a) * half, half)
                n2 = 10 + it
                rcopy(
                    tok.at[n, rows], tok.at[n2, rows], fw2_s.at[n - 4], tok_r.at[n2, 1 - a],
                    z, a2p if a == 1 else a2m,
                ).start()

        @pl.when(it >= 6)
        def _():
            for a in range(2):
                for h in range(2):
                    half_of(2 * it + a, h).wait_recv()

    s24 = lax.broadcasted_iota(jnp.int32, (CAP, TB), 0).astype(F32)

    def dsend(k, ee):
        return rcopy(
            sendbuf.at[k % 2, ee], dpar.at[k, ee], dp_s.at[k % 2, ee], dp_r.at[k, ee],
            z, partner,
        )

    def dispatch(it):
        n0 = 2 * it
        buf = it % 2
        code0, code1 = codes[n0], codes[n0 + 1]
        zero = jnp.zeros((CAP, TB), F32)
        blocks = []
        for q in range(4):
            b0 = jnp.where(jnp.abs(code0[q : q + 1, :] - s24) < 0.5, 1.0, 0.0)
            b1 = jnp.where(jnp.abs(code1[q : q + 1, :] - s24) < 0.5, 1.0, 0.0)
            blocks.append(jnp.concatenate([b0, zero], axis=1))
            blocks.append(jnp.concatenate([zero, b1], axis=1))
        pick = jnp.concatenate(blocks, axis=0).astype(BF16)

        @pl.when(it >= 2)
        def _():
            dsend(it, 0).wait_send()
            dsend(it, 1).wait_send()

        def tile(t, carry):
            cs = pl.ds(pl.multiple_of(t * 512, 512), 512)
            rows = tok[pl.ds(n0, 2), :, cs].reshape(2 * TB, 512)
            got = jnp.dot(pick, rows, preferred_element_type=F32).astype(BF16)
            down[0, :, cs] = got[0:48]
            down[1, :, cs] = got[48:96]
            sendbuf[buf, 0, :, cs] = got[96:144]
            sendbuf[buf, 1, :, cs] = got[144:192]
            return carry

        lax.fori_loop(0, D // 512, tile, 0)
        dsend(it, 0).start()
        dsend(it, 1).start()

    NT = (((1,), (1,)), ((), ()))

    def saved_rows(it):
        base = lax.broadcasted_iota(jnp.int32, (CAP, sg.shape[2]), 1) - lax.broadcasted_iota(
            jnp.int32, (CAP, sg.shape[2]), 0
        )
        blocks = []
        for o in range(2):
            cc = c if o == 0 else 1 - c
            for a in range(2):
                i, j = place(2 * it + a)
                blocks.append(jnp.where(base == dev(cc, i, j) * CAP, 1.0, 0.0))
        return jnp.concatenate(blocks, axis=0).astype(BF16)

    def hidden(it, ee, perm, eye):
        acc = jnp.zeros((96, F), F32)
        for kt in range(0, D, 512):
            rows = jnp.concatenate(
                [
                    down[ee, :, kt : kt + 512],
                    dpar[it, ee, :, kt : kt + 512],
                ],
                axis=0,
            )
            acc = acc + lax.dot_general(
                rows, wd[ee, :, kt : kt + 512], NT, preferred_element_type=F32
            )
        g = lax.dot_general(perm, sg[ee], NT, preferred_element_type=F32)
        u = lax.dot_general(perm, su[ee], NT, preferred_element_type=F32)
        s = 1.0 / (1.0 + jnp.exp(-g))
        silu = g * s
        router = jnp.sum(silu * u * acc, axis=1, keepdims=True)
        rown[it, ee : ee + 1, 0:96] = jnp.sum(router * eye, axis=0, keepdims=True)
        gus[ee, :, 0:F] = (acc * u * s * (1.0 + g * (1.0 - s))).astype(BF16)
        gus[ee, :, F : 2 * F] = (acc * silu).astype(BF16)

    def eye_of():
        return jnp.where(
            lax.broadcasted_iota(jnp.int32, (96, 96), 0)
            == lax.broadcasted_iota(jnp.int32, (96, 96), 1),
            1.0,
            0.0,
        )

    def rs_wait_send(buf):
        rcopy(
            rbuf.at[0], rbuf.at[0], rs_s.at[buf], rs_r.at[0, 0, 0], zp, e,
        ).wait_send()

    def partial(it, ee):
        buf = it % 3

        if ee == 0:
            @pl.when(it >= 3)
            def _():
                rs_wait_send(buf)

        gu = gus[ee]

        def tile(t, carry):
            cs = cols(t)
            v = jnp.dot(gu, wgu[ee, :, cs], preferred_element_type=F32)
            part[buf, ee, t] = v.astype(BF16)
            return carry

        lax.fori_loop(0, NZ, tile, 0)

    def router_copy(k, n):
        return rcopy(rown.at[k], rrecv.at[k, n - 1], rt_s.at[k], rt_r.at[k], (z + n) % NZ, e)

    def send_router(it):
        def go(n, carry):
            router_copy(it, n).start()
            return carry

        lax.fori_loop(1, NZ, go, 0)

    def work(it, h):
        if h == 0:
            for ee in range(2):
                dsend(it, ee).wait_recv()
            hidden(it, 0, saved_rows(it), eye_of())
        elif h == 1:
            hidden(it, 1, saved_rows(it), eye_of())
            send_router(it)
        elif h == 2:
            partial(it, 0)
        else:
            partial(it, 1)

    def fetch(it):
        arrive(it)
        dispatch(it)

    def rs_copy(k, s, d, ee):
        t = (z + 4 - s) % NZ if d == 0 else (z + 4 + s) % NZ
        n = 2 * s - 1 + ee if s else 0
        return rcopy(
            part.at[k % 3, ee, t], rbuf.at[k, d, n], rs_s.at[k % 3],
            rs_r.at[k, d, n], zp if d == 0 else zm, e,
        ), t, n

    def ring(k, s):
        order = [(ee, d) for ee in range(2) for d in range(2)]
        if s == 0:
            order = [(0, 0), (1, 1)]
        elif s == 1:
            order = [(1, 0), (0, 1), (0, 0), (1, 1)]
        for ee, d in order:
            cp, t, n = rs_copy(k, s, d, ee)
            if s > 1 or (s == 1 and ee == d):
                before, _, m = rs_copy(k, s - 1, d, ee)
                before.wait_recv()
                part[k % 3, ee, t] = (
                    part[k % 3, ee, t].astype(F32) + rbuf[k, d, m].astype(F32)
                ).astype(BF16)
            cp.start()

    def message(n, cc, i, j):
        return rcopy(fin.at[n], back.at[e], bk_s, bk_r, z, dev(cc, i, j))

    def finish(k):
        rcopy(rrecv.at[k], rrecv.at[k], rt_s.at[k], rt_r.at[k], zp, e).wait()
        rows = rown[k]
        for n in range(NZ - 1):
            rows = rows + rrecv[k, n]
        eye = eye_of()
        for ee in range(2):
            col = jnp.sum(rows[ee : ee + 1, 0:96] * eye, axis=1, keepdims=True)
            rcol[ee] = jnp.broadcast_to(col, (96, 128))
        got = []
        for ee in range(2):
            total = part[k % 3, ee, z].astype(F32)
            for d in range(2):
                last, _, m = rs_copy(k, 3, d, ee)
                last.wait_recv()
                total = total + rbuf[k, d, m].astype(F32)
            got.append(total)
        for o in range(2):
            cc = c if o == 0 else 1 - c
            for a in range(2):
                n = 4 * k + 2 * o + a
                lo_, hi_ = 48 * o + 24 * a, 48 * o + 24 * a + 24
                fin[n, :, 0:DS] = jnp.concatenate([got[0][lo_:hi_], got[1][lo_:hi_]], axis=0).astype(BF16)
                fin[n, :, DS : DS + 128] = jnp.concatenate(
                    [rcol[0, lo_:hi_], rcol[1, lo_:hi_]], axis=0
                ).astype(BF16)
                i, j = place(2 * k + a)
                if o == 0 and a == 0:
                    @pl.when(k == 0)
                    def _():
                        back[e] = fin[n]

                    @pl.when(k > 0)
                    def _():
                        message(n, cc, i, j).start()
                else:
                    message(n, cc, i, j).start()

    def step(it, carry):
        def when(lo_, hi_, fn, *args):
            @pl.when((it >= lo_) & (it <= hi_))
            def _():
                fn(*args)

        when(2, 9, ring, it - 2, 2)
        when(3, 10, finish, it - 3)
        when(9, 9, weights)
        when(1, 8, ring, it - 1, 1)
        when(0, 7, work, it, 0)
        when(0, 7, work, it, 1)
        when(0, 7, work, it, 2)
        when(2, 9, ring, it - 2, 3)
        when(0, 7, work, it, 3)
        when(0, 7, ring, it, 0)
        when(0, 6, fetch, it + 1)
        return carry

    dispatch(0)
    lax.fori_loop(0, 11, step, 0)

    rcopy(back.at[0:31], back.at[0:31], bk_s, bk_r, z, partner).wait()
    rows = back[:, :, 0:DS].reshape(LT, DS)
    out_ref[...] = (
        jnp.dot(whi[...], rows, preferred_element_type=F32)
        + jnp.dot(wlo[...], rows, preferred_element_type=F32)
    ).astype(BF16)
    off = lax.broadcasted_iota(jnp.int32, (LT, 128), 0) - CAP * lax.broadcasted_iota(
        jnp.int32, (LT, 128), 1
    )
    route = back[:, :, DS : DS + 128].reshape(LT, 128).astype(F32)
    route = jnp.where((off >= 0) & (off < CAP), route, 0.0).astype(BF16)
    vt = jnp.dot(onehot[...], route, preferred_element_type=F32).T
    for k in range(TOPK):
        gp_ref[k : k + 1, :] = jnp.sum(
            jnp.where(ids_ref[k : k + 1, :] == r128, vt, 0.0), axis=0, keepdims=True
        )

    for d in range(2):
        for s in range(4):
            for h in range(2):
                if s < 3 or h == d:
                    zsend(d, s, h).wait_send()
    rcopy(idsall.at[1:16], idsall.at[1:16], ids_s, ids_r, z, a1p).wait_send()
    for d in range(2):
        rcopy(tok.at[0], tok.at[1], st1_s.at[d], tok_r.at[1, 0], z, a1p).wait_send()
    fwd1_hi.wait_send()
    fwd1_lo.wait_send()
    for mi in range(4):
        for d in range(2):
            rcopy(tok.at[mi], tok.at[5], st2_s.at[mi, d], tok_r.at[5, 0], z, a2p).wait_send()
    for u in range(8):
        rcopy(tok.at[4, lo], tok.at[12, lo], fw2_s.at[u], tok_r.at[12, 0], z, a2p).wait_send()
    for k in range(2):
        for ee in range(2):
            dsend(k, ee).wait_send()
    for buf in range(3):
        rs_wait_send(buf)


def local(grad_out, probs, expert_ids, w_gate, w_up, w_down, saved_gate, saved_up):
    D, F, S = w_gate.shape[2], w_gate.shape[1], saved_gate.shape[2]
    DS = D // NZ
    vm = pl.BlockSpec(memory_space=pltpu.VMEM)
    hbm = pl.BlockSpec(memory_space=pl.ANY)
    dma = pltpu.SemaphoreType.DMA
    out, gp = pl.pallas_call(
        kernel,
        out_shape=(
            jax.ShapeDtypeStruct((TB, DS), BF16),
            jax.ShapeDtypeStruct((TOPK, TB), F32),
        ),
        in_specs=[vm, vm] + [hbm] * 6,
        out_specs=(vm, vm),
        scratch_shapes=[
            pltpu.VMEM((16, TB, D), BF16),
            pltpu.VMEM((2, 2 * F, D), BF16),
            pltpu.VMEM((2, F, D), BF16),
            pltpu.VMEM((2, F, S), BF16),
            pltpu.VMEM((2, F, S), BF16),
            pltpu.VMEM((2, 48, D), BF16),
            pltpu.VMEM((8, 2, 48, D), BF16),
            pltpu.VMEM((2, 2, 48, D), BF16),
            pltpu.VMEM((3, 2, NZ, 96, DS), BF16),
            pltpu.VMEM((8, 2, NZ - 1, 96, DS), BF16),
            pltpu.VMEM((32, 48, DS + 128), BF16),
            pltpu.VMEM((32, 48, DS + 128), BF16),
            pltpu.VMEM((16, TOPK, TB), jnp.int32),
            pltpu.VMEM((16, 8, TB), F32),
            pltpu.VMEM((16, 8, TB), F32),
            pltpu.VMEM((8, 8, 128), F32),
            pltpu.VMEM((8, NZ - 1, 8, 128), F32),
            pltpu.VMEM((2, 96, 128), F32),
            pltpu.VMEM((TB, 1536), BF16),
            pltpu.VMEM((TB, 1536), BF16),
            pltpu.VMEM((TB, 1536), BF16),
            pltpu.VMEM((2, 96, 2 * F), BF16),
            dma((6,)),
            dma,
            dma((2, 4, 2)),
            dma((2, 4, 2)),
            dma,
            dma,
            dma((2,)),
            dma((2,)),
            dma((4, 2)),
            dma((8,)),
            dma((16, 2)),
            dma((2, 2)),
            dma((8, 2)),
            dma((3,)),
            dma((8, 2, NZ - 1)),
            dma((8,)),
            dma((8,)),
            dma,
            dma,
        ],
        compiler_params=pltpu.CompilerParams(
            collective_id=0, has_side_effects=True, vmem_limit_bytes=67043328
        ),
    )(expert_ids.T, probs.T, grad_out, w_gate, w_up, w_down, saved_gate, saved_up)
    return out, gp.astype(BF16).T


def solution(mesh):
    placed = (
        P("expert", "section"),
        P("expert", None),
        P("expert", None),
        P("expert", "section", None),
        P("expert", "section", None),
        P("expert", "section", None),
        P("expert", "section", None),
        P("expert", "section", None),
    )
    return jax.shard_map(
        local,
        mesh=mesh,
        in_specs=placed,
        out_specs=(P("expert", "section"), P("expert", None)),
        check_vma=False,
    )
```
